128 devices in a mesh: row: 8 (over x, core), col: 16 (over z, y).
Axes of the slice: x: 4, y: 4, z: 4, core: 2. Of those that a mesh axis runs over, the one named last changes fastest.
Arguments:
- embeddings: bfloat16 [32768, 1024], P(('row', 'col')), may hold values from -6 to 6
- features: bfloat16 [32768, 256], P(('row', 'col')), may hold values from -6 to 6
- candidates: int32 [256, 38], P(('row', 'col')), may hold values from 0 to 255, as said below
Outputs:
- smoothed: bfloat16 [32768, 256], P(('row', 'col'))
The draws below stay inside these ranges and needn't reach their ends.
Inputs may be any that keep to these rules, and one draw needn't show every extreme that they name: `candidates`: each row names 38 distinct blocks. Over the blocks held by one row of devices, the entries that name blocks held by one column of devices number at most 160, and in every row of devices some column reaches that number.
All inputs are finite; a program needn't handle non-finite values.
Results may differ from the reference program's by a relative error of at most 0.012.
The reference program's roundings to bfloat16 on the way count: a program that leaves them out, or rounds other values in their place, can miss the bound.
Values may be sent and summed in bfloat16 or wider, within the bound.
No kernel may reach another device: no remote copies, remote signals or barrier semaphores. Data moves between devices by JAX's collectives and lax.ppermute only.
A program may use at most 128 MiB of HBM per device.

```python
import jax
import jax.numpy as jnp
import numpy as np
from jax import lax

EMB = 1024
FEAT = 256
BLOCK = 128
NB_DEV = 2
HOT = 8
BASE = 2
BETA = 16
GROUPS = 16
GROUP_BLOCKS = 16
NBLK = 256
DOCS = 32768
K = 38


def draw_embeddings(key, part):
    first = jax.random.fold_in(key, 0)
    column = jnp.arange(EMB, dtype=jnp.float32)
    factor = lax.rsqrt(column + 1.0)
    values = jax.random.truncated_normal(first, -6.0, 6.0, (DOCS, EMB), jnp.float32) * factor[None, :]
    return values.astype(jnp.bfloat16)


def draw_candidates(key, part):
    hot_key, perm_key = jax.random.split(jax.random.fold_in(key, 17))
    block_ids = jnp.arange(NBLK, dtype=jnp.int32)
    holder = block_ids // NB_DEV
    row_group = holder // GROUPS
    within = block_ids % (GROUPS * NB_DEV)
    row_groups = NBLK // (GROUPS * NB_DEV)
    hot_start = jax.random.randint(hot_key, (row_groups,), 0, GROUPS, dtype=jnp.int32)
    hot_group = (hot_start[row_group] + within % 2) % GROUPS
    slots = np.arange(K)
    group_offset = np.where(slots < HOT, 0, 1 + (slots - HOT) // BASE).astype(np.int32)
    slot_index = np.where(slots < HOT, slots, (slots - HOT) % BASE).astype(np.int32)
    group = (hot_group[:, None] + jnp.asarray(group_offset)[None, :]) % GROUPS
    keys = jax.random.split(perm_key, NBLK * GROUPS)
    perms = jax.vmap(lambda single: jax.random.permutation(single, GROUP_BLOCKS))(keys)
    perms = perms.astype(jnp.int32).reshape(NBLK, GROUPS, GROUP_BLOCKS)
    chosen = perms[block_ids[:, None], group, jnp.asarray(slot_index)[None, :]]
    return ((chosen // NB_DEV * GROUPS + group) * NB_DEV + chosen % NB_DEV).astype(jnp.int32)


def level_of(stream_key, dims, shards, smallest, largest):
    def one(dim, parts):
        draws = jax.random.uniform(jax.random.fold_in(jax.random.fold_in(stream_key, 6), dim), (parts,), jnp.float32, smallest / len(shards), largest / len(shards))
        return jnp.repeat(jnp.exp(draws), dims[dim] // parts).reshape((-1,) + (1,) * (len(dims) - dim - 1))

    factor_of = one(*shards[0])
    for cut in shards[1:]:
        factor_of = factor_of * one(*cut)
    return factor_of


def normal_values(key, dims, spread, bound, cuts=(), kind=jnp.bfloat16):
    loudness = level_of(key, dims, cuts, -0.22, 0.18) if cuts else 1.0
    values = jax.random.normal(key, dims, jnp.float32) * spread * loudness
    return jnp.minimum(jnp.maximum(values, -bound), bound).astype(kind)


def setup_inputs(seed: int = 0) -> dict:
    key_list = jax.random.split(jax.random.key(seed), 4)
    return {
        "embeddings": draw_embeddings(jax.random.fold_in(key_list[3], 71), 0),
        "features": normal_values(key_list[1], (DOCS, FEAT), 1.0, 6.0, ((0, 128),)),
        "candidates": draw_candidates(jax.random.fold_in(key_list[3], 71), 0),
    }


def unit_rows(embeddings):
    values = embeddings.astype(jnp.float32)
    factor = lax.rsqrt(lax.optimization_barrier(jnp.mean(values * values, axis=1, keepdims=True)) + 1e-06) * values.shape[1] ** (-0.5)
    return (values * factor).astype(jnp.bfloat16)

def reference(embeddings, features, candidates):
    units = unit_rows(embeddings)
    blocks = candidates.shape[0]
    unit_blocks = units.reshape(blocks, BLOCK, EMB)
    feat_blocks = features.reshape(blocks, BLOCK, FEAT)
    diagonal_mask = jnp.eye(BLOCK, dtype=jnp.bool_)

    def one_block(index):
        names = candidates[index]
        query = unit_blocks[index].astype(jnp.float32)
        cand_units = jnp.take(unit_blocks, names, axis=0).astype(jnp.float32)
        cosine = jnp.einsum('ie,kje->ikj', query, cand_units)
        weight = jnp.exp(BETA * (cosine - 1.0))
        is_self = jnp.logical_and((names == index)[None, :, None], diagonal_mask[:, None, :])
        weight = jnp.where(is_self, jnp.float32(0.0), weight)
        denominator = lax.optimization_barrier(jnp.sum(weight, axis=(1, 2)))
        rounded = lax.optimization_barrier(weight.astype(jnp.bfloat16))
        cand_feats = jnp.take(feat_blocks, names, axis=0).astype(jnp.float32)
        numerator = jnp.einsum('ikj,kjf->if', rounded.astype(jnp.float32), cand_feats)
        return (numerator / denominator[:, None]).astype(jnp.bfloat16)
    result = lax.map(one_block, jnp.arange(blocks, dtype=jnp.int32))
    return result.reshape(blocks * BLOCK, FEAT)
```

```python
import functools

import jax
import jax.numpy as jnp
from jax import lax
from jax.experimental import pallas as pl
from jax.experimental.pallas import tpu as pltpu
from jax.sharding import PartitionSpec as P

EMB = 1024
FEAT = 256
BLOCK = 128
NB_DEV = 2
BETA = 16
DOCS_DEV = NB_DEV * BLOCK
LIST_ROWS = 16
AXES = ("row", "col")
VALID, SELF = 1 << 11, 1 << 10


def hop(dx=0, dz=0, flip_core=False, y_of=lambda y: y):
    pairs = []
    for x in range(4):
        for k in range(2):
            for z in range(4):
                for y in range(4):
                    x2, k2, z2, y2 = (x + dx) % 4, (1 - k if flip_core else k), (z + dz) % 4, y_of(y)
                    pairs.append(((2 * x + k) * 16 + 4 * z + y, (2 * x2 + k2) * 16 + 4 * z2 + y2))
    return pairs


def partner_a(y):
    return y ^ 1


def partner_b(y):
    return 3 - y


def send(value, **where):
    return lax.ppermute(value, AXES, hop(**where))


def units_kernel(emb_ref, feat_ref, list_ref, unit_ref, cand_ref):
    values = emb_ref[...].astype(jnp.float32)
    factor = lax.rsqrt(jnp.mean(values * values, axis=1, keepdims=True) + 1e-06) * EMB ** (-0.5)
    units = (values * factor).astype(jnp.bfloat16)
    unit_ref[pl.ds(0, DOCS_DEV), :] = units
    unit_ref[pl.ds(DOCS_DEV, LIST_ROWS), :] = list_ref[...]
    cand_ref[:, pl.ds(0, EMB)] = units
    cand_ref[:, pl.ds(EMB, FEAT)] = feat_ref[...]


def unit_payloads(embeddings, features, candidates):
    rows = jnp.pad(
        candidates.astype(jnp.bfloat16),
        ((0, LIST_ROWS - candidates.shape[0]), (0, EMB - candidates.shape[1])),
    )
    return pl.pallas_call(
        units_kernel,
        out_shape=(
            jax.ShapeDtypeStruct((DOCS_DEV + LIST_ROWS, EMB), jnp.bfloat16),
            jax.ShapeDtypeStruct((DOCS_DEV, EMB + FEAT), jnp.bfloat16),
        ),
        name="units",
    )(embeddings, features, rows)


def pair_codes(lists, query_ids, cand_ids):
    member = jnp.any(lists[:, :, None] == cand_ids[None, None, :], axis=1)
    queries, cands = member.shape
    total = queries * cands
    same = query_ids[:, None] == cand_ids[None, :]
    code = (
        jnp.arange(queries, dtype=jnp.int32)[:, None]
        + 32 * jnp.arange(cands, dtype=jnp.int32)[None, :]
        + jnp.where(same, SELF, 0)
        + VALID
    )
    member, code = member.T.reshape(total), code.T.reshape(total)
    position = jnp.arange(total, dtype=jnp.int32)
    rank = jnp.sum(jnp.where(position[None, :] < position[:, None], member[None, :], False).astype(jnp.int32), axis=1)
    hit = jnp.logical_and(member[None, :], rank[None, :] == position[:, None])
    return jnp.sum(jnp.where(hit, code[None, :], 0), axis=1), jnp.sum(member.astype(jnp.int32)).reshape(1)


UNROLL = 4


def smooth_kernel(nq, nc, first, last, *refs):
    codes, count = refs[:2]
    q_in, c_in = refs[2 : 2 + nq], refs[2 + nq : 2 + nq + nc]
    at = 2 + nq + nc
    if not first:
        num_in, den_in = refs[at : at + 2]
        at += 2
    num_out, den_out = refs[at : at + 2]
    at += 2
    if last:
        num, den = refs[at : at + 2]
        at += 2
    else:
        num, den = num_out, den_out
    q_buf, c_buf, sems = refs[at:]
    copies = []
    for i, ref in enumerate(q_in):
        copies.append(
            pltpu.make_async_copy(
                ref.at[pl.ds(0, DOCS_DEV), :], q_buf.at[pl.ds(i * DOCS_DEV, DOCS_DEV), :], sems.at[i]
            )
        )
    for i, ref in enumerate(c_in):
        copies.append(
            pltpu.make_async_copy(ref, c_buf.at[pl.ds(i * DOCS_DEV, DOCS_DEV), :], sems.at[nq + i])
        )
    for copy in copies:
        copy.start()
    if first:
        num[...] = jnp.zeros_like(num)
        den[...] = jnp.zeros_like(den)
    elif last:
        num[...] = num_in[...]
        den[...] = den_in[...]
    for copy in copies:
        copy.wait()
    rows = lax.broadcasted_iota(jnp.int32, (BLOCK, BLOCK), 0)
    cols = lax.broadcasted_iota(jnp.int32, (BLOCK, BLOCK), 1)
    diagonal = rows == cols

    def turn(i, carry):
        for u in range(UNROLL):
            code = codes[i * UNROLL + u]
            at_q = pl.ds(pl.multiple_of((code & 31) * BLOCK, BLOCK), BLOCK)
            at_c = pl.ds(pl.multiple_of(((code >> 5) & 31) * BLOCK, BLOCK), BLOCK)
            cosine = lax.dot_general(
                q_buf[at_q, :],
                c_buf[at_c, pl.ds(0, EMB)],
                (((1,), (1,)), ((), ())),
                preferred_element_type=jnp.float32,
            )
            weight = jnp.exp(BETA * (cosine - 1.0))
            drop = jnp.logical_or(code < VALID, jnp.logical_and((code & SELF) > 0, diagonal))
            weight = jnp.where(drop, 0.0, weight)
            den[at_q, :] += weight
            num[at_q, :] += jnp.dot(
                weight.astype(jnp.bfloat16),
                c_buf[at_c, pl.ds(EMB, FEAT)],
                preferred_element_type=jnp.float32,
            )
        return carry

    lax.fori_loop(0, (count[0] + UNROLL - 1) // UNROLL, turn, 0)
    if last:
        num_out[...] = num[...]
        ones = jnp.ones((8, BLOCK), jnp.float32)
        for b in range(nq * NB_DEV):
            sums = lax.dot_general(
                ones,
                den[pl.ds(b * BLOCK, BLOCK), :],
                (((1,), (1,)), ((), ())),
                preferred_element_type=jnp.float32,
                precision=lax.Precision.HIGHEST,
            )
            den_out[pl.ds(8 * b, 8), :] = sums


def smooth(codes, count, queries, cands, state, last):
    nq, nc = len(queries), len(cands)
    first = state is None
    docs = nq * DOCS_DEV
    hbm, vmem, smem = (
        pl.BlockSpec(memory_space=pl.ANY),
        pl.BlockSpec(memory_space=pltpu.VMEM),
        pl.BlockSpec(memory_space=pltpu.SMEM),
    )
    scratch = []
    if last:
        scratch = [pltpu.VMEM((docs, FEAT), jnp.float32), pltpu.VMEM((docs, BLOCK), jnp.float32)]
    den_shape = (nq * NB_DEV * 8, BLOCK) if last else (docs, BLOCK)
    return pl.pallas_call(
        functools.partial(smooth_kernel, nq, nc, first, last),
        in_specs=[smem, smem] + [hbm] * (nq + nc) + ([] if first else [vmem, vmem]),
        out_specs=(vmem, vmem),
        out_shape=(
            jax.ShapeDtypeStruct((docs, FEAT), jnp.float32),
            jax.ShapeDtypeStruct(den_shape, jnp.float32),
        ),
        scratch_shapes=scratch
        + [
            pltpu.VMEM((docs, EMB), jnp.bfloat16),
            pltpu.VMEM((nc * DOCS_DEV, EMB + FEAT), jnp.bfloat16),
            pltpu.SemaphoreType.DMA((nq + nc,)),
        ],
        compiler_params=pltpu.CompilerParams(vmem_limit_bytes=48 << 20),
        cost_estimate=pl.CostEstimate(
            flops=40 * 2 * BLOCK * BLOCK * (EMB + FEAT),
            bytes_accessed=nq * DOCS_DEV * EMB * 2 + nc * DOCS_DEV * (EMB + FEAT) * 2,
            transcendentals=40 * BLOCK * BLOCK,
        ),
        name="smooth_last" if last else "smooth",
    )(codes, count, *queries, *cands, *(state or ()))


def on_device(embeddings, features, candidates):
    row, col = lax.axis_index("row"), lax.axis_index("col")
    x, k, z, y = row // 2, row % 2, col // 4, col % 4
    units, cand = unit_payloads(embeddings, features, candidates)

    def blocks_of(x, k, z, y):
        device = (2 * (x % 4) + k) * 16 + 4 * (z % 4) + y
        return [device * NB_DEV + b for b in range(NB_DEV)]

    c_b = send(cand, y_of=partner_b)
    c_r, c_l, c_o = send(cand, dz=1), send(cand, dz=-1), send(cand, dz=2)
    q_r, q_l, q_a, q_o = (
        send(units, dx=1),
        send(units, dx=-1),
        send(units, y_of=partner_a),
        send(units, dx=2),
    )
    c_br, c_bl, c_bo = send(c_b, dz=1), send(c_b, dz=-1), send(c_o, y_of=partner_b)
    q_ar, q_al, q_ao = send(q_a, dx=1), send(q_a, dx=-1), send(q_o, y_of=partner_a)
    queries = [units, q_r, q_l, q_o, q_a, q_ar, q_al, q_ao]
    ya, yb = partner_a(y), partner_b(y)
    q_from = [(0, y), (-1, y), (1, y), (2, y), (0, ya), (-1, ya), (1, ya), (2, ya)]
    query_ids = jnp.stack([b for dx, yy in q_from for b in blocks_of(x + dx, k, z, yy)])
    lists = jnp.concatenate(
        [q[DOCS_DEV : DOCS_DEV + NB_DEV, : candidates.shape[1]] for q in queries], axis=0
    ).astype(jnp.int32)

    early = [cand, c_b, c_r, c_l]
    late = [c_o, c_br, c_bl, c_bo]
    early_from = [(0, y), (0, yb), (-1, y), (1, y)]
    late_from = [(2, y), (-1, yb), (1, yb), (2, yb)]
    state = None
    for group, source, last in ((early, early_from, False), (late, late_from, True)):
        other = [send(c, flip_core=True) for c in group]
        cand_ids = jnp.stack(
            [b for kk in (k, 1 - k) for dz, yy in source for b in blocks_of(x, kk, z + dz, yy)]
        )
        codes, count = pair_codes(lists, query_ids, cand_ids)
        state = smooth(codes, count, queries, group + other, state, last)
    numerator, sums = state
    numerator = numerator.reshape(len(queries), DOCS_DEV, FEAT)
    sums = sums.reshape(len(queries), NB_DEV, 8, BLOCK)[:, :, 0, :].reshape(len(queries), 1, DOCS_DEV)
    high = sums.astype(jnp.bfloat16)
    low = (sums - high.astype(jnp.float32)).astype(jnp.bfloat16)
    payload = jnp.concatenate(
        [numerator.astype(jnp.bfloat16), high, low, jnp.zeros((len(queries), 14, FEAT), jnp.bfloat16)],
        axis=1,
    )
    home = [
        dict(dx=-1), dict(dx=1), dict(dx=2), dict(y_of=partner_a),
        dict(dx=-1, y_of=partner_a), dict(dx=1, y_of=partner_a), dict(dx=2, y_of=partner_a),
    ]
    back = [send(payload[1 + i], **where) for i, where in enumerate(home)]
    top, bottom = numerator[0], sums[0]
    for part in back:
        part = part.astype(jnp.float32)
        top = top + part[:DOCS_DEV]
        bottom = bottom + part[DOCS_DEV : DOCS_DEV + 1] + part[DOCS_DEV + 1 : DOCS_DEV + 2]
    return (top / bottom.reshape(DOCS_DEV, 1)).astype(jnp.bfloat16)


def solution(mesh):
    spec = P(("row", "col"), None)
    return jax.shard_map(
        on_device, mesh=mesh, in_specs=(spec, spec, spec), out_specs=spec, check_vma=False
    )
```

```python
import functools

import jax
import jax.numpy as jnp
from jax import lax
from jax.experimental import pallas as pl
from jax.experimental.pallas import tpu as pltpu
from jax.sharding import PartitionSpec as P


EMB = 1024
FEAT = 256
BLOCK = 128
NB_DEV = 2
BETA = 16
DOCS_DEV = NB_DEV * BLOCK
LIST_ROWS = 16
AXES = ("row", "col")
VALID, SELF = 1 << 11, 1 << 10


def hop(dx=0, dz=0, flip_core=False, y_of=lambda y: y):
    pairs = []
    for x in range(4):
        for k in range(2):
            for z in range(4):
                for y in range(4):
                    x2, k2, z2, y2 = (x + dx) % 4, (1 - k if flip_core else k), (z + dz) % 4, y_of(y)
                    pairs.append(((2 * x + k) * 16 + 4 * z + y, (2 * x2 + k2) * 16 + 4 * z2 + y2))
    return pairs


def partner_a(y):
    return y ^ 1


def partner_b(y):
    return 3 - y


def send(value, **where):
    return lax.ppermute(value, AXES, hop(**where))


def cand_kernel(emb_ref, feat_ref, cand_ref):
    values = emb_ref[...].astype(jnp.float32)
    factor = lax.rsqrt(jnp.mean(values * values, axis=1, keepdims=True) + 1e-06) * EMB ** (-0.5)
    cand_ref[:, pl.ds(0, EMB)] = (values * factor).astype(jnp.bfloat16)
    cand_ref[:, pl.ds(EMB, FEAT)] = feat_ref[...]


def query_kernel(unit_ref, own_ref, partner_ref, query_ref):
    query_ref[pl.ds(0, DOCS_DEV), :] = unit_ref[...]
    query_ref[pl.ds(DOCS_DEV, LIST_ROWS), :] = jnp.zeros((LIST_ROWS, EMB), jnp.bfloat16)
    for lane, ref in ((0, own_ref), (BLOCK, partner_ref)):
        lists, length = ref.shape
        query_ref[pl.ds(DOCS_DEV, lists), pl.ds(lane, length)] = (
            ref[...].astype(jnp.float32).astype(jnp.bfloat16)
        )


def small(limit=8):
    return pltpu.CompilerParams(vmem_limit_bytes=limit << 20)


def cand_payload(embeddings, features):
    return pl.pallas_call(
        cand_kernel,
        out_shape=jax.ShapeDtypeStruct((DOCS_DEV, EMB + FEAT), jnp.bfloat16),
        name="cand",
    )(embeddings, features)


def query_payload(cand, own, partner):
    return pl.pallas_call(
        query_kernel,
        grid=(1,),
        in_specs=[
            pl.BlockSpec((DOCS_DEV, EMB), lambda i: (0, 0)),
            pl.BlockSpec(own.shape, lambda i: (0, 0)),
            pl.BlockSpec(partner.shape, lambda i: (0, 0)),
        ],
        out_specs=pl.BlockSpec((DOCS_DEV + LIST_ROWS, EMB), lambda i: (0, 0)),
        out_shape=jax.ShapeDtypeStruct((DOCS_DEV + LIST_ROWS, EMB), jnp.bfloat16),
        name="query",
    )(cand, own, partner)


Q_FROM = ((0, 0), (-1, 0), (1, 0), (0, 1), (2, 0), (-1, 1), (1, 1), (2, 1))
LATE_FROM, EARLY_FROM = ((-1, 1), (1, 1)), ((0, 0), (0, 1), (2, 0), (-1, 0), (1, 0), (2, 1))
C_FROM = tuple((core, *f) for group in (LATE_FROM, EARLY_FROM) for core in (0, 1) for f in group)
Q_EARLY = 5
N_LATE, N_EARLY = 2 * len(LATE_FROM), 2 * len(EARLY_FROM)
SLOTS, COUNT = 384, 376


def codes_kernel(own_ref, partner_ref, r_ref, l_ref, o_ref, out_ref, stage, lists, sems):
    copies = [
        pltpu.make_async_copy(ref.at[pl.ds(DOCS_DEV, LIST_ROWS), pl.ds(0, 2 * BLOCK)], stage.at[i], sems.at[i])
        for i, ref in enumerate((r_ref, l_ref, o_ref))
    ]
    for copy in copies:
        copy.start()
    length = own_ref.shape[1]
    lists[...] = jnp.full_like(lists, -1.0)
    lists[pl.ds(0, 2), pl.ds(0, length)] = own_ref[...].astype(jnp.float32)
    lists[pl.ds(6, 2), pl.ds(0, length)] = partner_ref[...].astype(jnp.float32)
    for copy in copies:
        copy.wait()
    for i, (own_at, partner_at) in enumerate(((2, 10), (4, 12), (8, 14))):
        values = stage[i].astype(jnp.float32)
        lists[pl.ds(own_at, 2), pl.ds(0, length)] = values[0:2, 0:length]
        lists[pl.ds(partner_at, 2), pl.ds(0, length)] = values[0:2, BLOCK : BLOCK + length]
    named = lists[...]
    queries = named.shape[0]

    row, col = lax.axis_index("row"), lax.axis_index("col")
    x, k, z, y = row >> 1, row & 1, col >> 2, col & 3
    lane = lax.broadcasted_iota(jnp.int32, (1, BLOCK), 1)
    ids = jnp.full((1, BLOCK), -2, jnp.int32)
    for i, (core, dz, partner) in enumerate(C_FROM):
        yy = 3 - y if partner else y
        kk = 1 - k if core else k
        device = (2 * x + kk) * 16 + ((z + dz) & 3) * 4 + yy
        ids = jnp.where((lane >> 1) == i, device * NB_DEV + (lane & 1), ids)

    blocks = lax.broadcasted_iota(jnp.int32, (queries, 256), 1).astype(jnp.float32)
    onehot = jnp.zeros((queries, 256), jnp.float32)
    for i in range(length):
        onehot = jnp.where(named[:, i : i + 1] == blocks, 1.0, onehot)
    chosen = jnp.where(lax.broadcasted_iota(jnp.int32, (256, BLOCK), 0) == ids, 1.0, 0.0)
    member = jnp.dot(
        onehot.astype(jnp.bfloat16), chosen.astype(jnp.bfloat16), preferred_element_type=jnp.float32
    )
    ahead = jnp.where(
        lax.broadcasted_iota(jnp.int32, (BLOCK, BLOCK), 0) < lax.broadcasted_iota(jnp.int32, (BLOCK, BLOCK), 1),
        1.0,
        0.0,
    ).astype(jnp.bfloat16)
    above = jnp.where(
        lax.broadcasted_iota(jnp.int32, (queries, queries), 0)
        > lax.broadcasted_iota(jnp.int32, (queries, queries), 1),
        1.0,
        0.0,
    ).astype(jnp.bfloat16)
    query = lax.broadcasted_iota(jnp.int32, (queries, BLOCK), 0)
    cand = lax.broadcasted_iota(jnp.int32, (queries, BLOCK), 1)
    old_query = query < Q_EARLY * NB_DEV
    late_end, half = N_LATE * NB_DEV, (N_LATE + N_EARLY // 2) * NB_DEV
    first_half = jnp.logical_and(cand >= late_end, cand < half)
    calls = (
        (jnp.logical_and(old_query, first_half), jnp.logical_and(old_query, cand >= half)),
        (cand < late_end, jnp.logical_and(jnp.logical_not(old_query), cand >= late_end)),
    )
    slot = lax.broadcasted_iota(jnp.int32, (1, SLOTS), 1)
    slots = slot.astype(jnp.float32)
    places = (N_LATE + N_EARLY) * NB_DEV
    place = lax.broadcasted_iota(jnp.int32, (places, 1), 0)
    for call, groups in enumerate(calls):
        base = jnp.zeros((1, 1), jnp.float32)
        position = jnp.full((queries, BLOCK), -1.0, jnp.float32)
        totals = []
        for group in groups:
            inside = jnp.where(group, member, 0.0)
            bits = inside.astype(jnp.bfloat16)
            in_row = jnp.dot(bits, ahead, preferred_element_type=jnp.float32)
            rows_above = jnp.sum(
                jnp.dot(above, bits, preferred_element_type=jnp.float32), axis=1, keepdims=True
            )
            position = jnp.where(inside > 0.0, base + rows_above + in_row, position)
            base = base + jnp.sum(jnp.sum(inside, axis=1, keepdims=True), axis=0, keepdims=True)
            totals.append(base)
        by_cand = jnp.concatenate(
            [position, jnp.full((BLOCK - queries, BLOCK), -1.0, jnp.float32)], axis=0
        ).T
        found = jnp.zeros((places, SLOTS), jnp.float32)
        first_place = 0 if call else late_end
        for q in range(queries):
            code = q + 32 * (place - first_place) + VALID
            if q < NB_DEV:
                code = code + jnp.where(place == late_end + q, SELF, 0)
            found = jnp.where(by_cand[0:places, q : q + 1] == slots, code.astype(jnp.float32), found)
        line = jnp.sum(found, axis=0, keepdims=True)
        line = jnp.where(slot == COUNT, totals[1], jnp.where(slot == COUNT + 1, totals[0], line))
        out_ref[pl.ds(call, 1), :] = line.astype(jnp.int32)


def pair_codes(own, partner, q_r, q_l, q_o):
    free, vmem = pl.BlockSpec(memory_space=pl.ANY), pl.BlockSpec(memory_space=pltpu.VMEM)
    return pl.pallas_call(
        codes_kernel,
        in_specs=[vmem, vmem, free, free, free],
        out_specs=vmem,
        out_shape=jax.ShapeDtypeStruct((2, SLOTS), jnp.int32),
        scratch_shapes=[
            pltpu.VMEM((3, LIST_ROWS, 2 * BLOCK), jnp.bfloat16),
            pltpu.VMEM((len(Q_FROM) * NB_DEV, BLOCK), jnp.float32),
            pltpu.SemaphoreType.DMA((3,)),
        ],
        compiler_params=small(),
        name="codes",
    )(own, partner, q_r, q_l, q_o)


UNROLL = 8
QUERIES = 8


def smooth_kernel(nq, nc, own, first_cands, last, *refs):
    codes = refs[0]
    q_in, c_in = refs[1 : 1 + nq], refs[1 + nq : 1 + nq + nc]
    num, den, q_buf, c_buf, sems = refs[-5:]
    state = refs[1 + nq + nc : 3 + nq + nc]
    old = state[0].shape[0]
    copies = []

    def load(source, target):
        copies.append(pltpu.make_async_copy(source, target, sems.at[len(copies)]))
        copies[-1].start()

    load(c_in[own].at[:, pl.ds(0, EMB)], q_buf.at[pl.ds(0, DOCS_DEV), :])
    for i, ref in enumerate(q_in):
        load(ref.at[pl.ds(0, DOCS_DEV), :], q_buf.at[pl.ds((i + 1) * DOCS_DEV, DOCS_DEV), :])
    if last:
        load(state[0], num.at[pl.ds(0, old), :])
        load(state[1], den.at[pl.ds(0, old), :])
    for i, ref in enumerate(c_in):
        load(ref, c_buf.at[pl.ds(i * DOCS_DEV, DOCS_DEV), :])
    fresh = pl.ds(old, num.shape[0] - old) if last else pl.ds(0, old)
    num[fresh, :] = jnp.zeros((fresh.size, FEAT), jnp.float32)
    den[fresh, :] = jnp.zeros((fresh.size, BLOCK), jnp.float32)
    waited = len(copies) - nc + first_cands
    for copy in copies[:waited]:
        copy.wait()
    diagonal = lax.broadcasted_iota(jnp.int32, (BLOCK, BLOCK), 0) == lax.broadcasted_iota(
        jnp.int32, (BLOCK, BLOCK), 1
    )
    call = 1 if last else 0

    def turn(i, carry):
        pairs = []
        for u in range(UNROLL):
            code = codes[call, i * UNROLL + u]
            at_q = pl.ds(pl.multiple_of((code & 31) * BLOCK, BLOCK), BLOCK)
            at_c = pl.ds(pl.multiple_of(((code >> 5) & 31) * BLOCK, BLOCK), BLOCK)
            pairs.append((code, at_q, at_c))
        cosines = [
            lax.dot_general(
                q_buf[at_q, :],
                c_buf[at_c, pl.ds(0, EMB)],
                (((1,), (1,)), ((), ())),
                preferred_element_type=jnp.float32,
            )
            for _, at_q, at_c in pairs
        ]
        weights = []
        for (code, _, _), cosine in zip(pairs, cosines):
            weight = jnp.exp(BETA * (cosine - 1.0))
            drop = jnp.logical_or(code < VALID, jnp.logical_and((code & SELF) > 0, diagonal))
            weights.append(jnp.where(drop, 0.0, weight))
        terms = [
            jnp.dot(
                weight.astype(jnp.bfloat16),
                c_buf[at_c, pl.ds(EMB, FEAT)],
                preferred_element_type=jnp.float32,
            )
            for (_, _, at_c), weight in zip(pairs, weights)
        ]
        for (_, at_q, _), weight, term in zip(pairs, weights, terms):
            den[at_q, :] += weight
            num[at_q, :] += term
        return carry

    ready = codes[call, COUNT + 1] // UNROLL
    lax.fori_loop(0, ready, turn, 0)
    for copy in copies[waited:]:
        copy.wait()
    lax.fori_loop(ready, (codes[call, COUNT] + UNROLL - 1) // UNROLL, turn, 0)
    if not last:
        for i, (source, target) in enumerate(((num, state[0]), (den, state[1]))):
            pltpu.make_async_copy(source, target, sems.at[i]).start()
        for i, (source, target) in enumerate(((num, state[0]), (den, state[1]))):
            pltpu.make_async_copy(source, target, sems.at[i]).wait()
        return
    payloads = refs[3 + nq + nc : -5]
    ones = jnp.ones((8, BLOCK), jnp.bfloat16)

    def lane_sums(part):
        return lax.dot_general(ones, part, (((1,), (1,)), ((), ())), preferred_element_type=jnp.float32)

    for i, payload in enumerate(payloads):
        docs = pl.ds(i * DOCS_DEV, DOCS_DEV)
        payload[pl.ds(0, DOCS_DEV), :] = num[docs, :].astype(jnp.bfloat16)
        weights = den[docs, :]
        high = weights.astype(jnp.bfloat16)
        middle = (weights - high.astype(jnp.float32)).astype(jnp.bfloat16)
        sums = lane_sums(high) + lane_sums(middle)
        high = sums.astype(jnp.bfloat16).astype(jnp.float32)
        pair = jnp.concatenate([high, sums - high], axis=0).astype(jnp.bfloat16)
        payload[pl.ds(DOCS_DEV, 16), :] = pair


def smooth(codes, queries, cands, own, first_cands, state):
    docs, last = (1 + len(queries)) * DOCS_DEV, state is not None
    free, hbm, vmem, smem = (
        pl.BlockSpec(memory_space=space) for space in (pl.ANY, pltpu.HBM, pltpu.VMEM, pltpu.SMEM)
    )
    operands = [codes, *queries, *cands, *(state or ())]
    if last:
        shapes = [jax.ShapeDtypeStruct((DOCS_DEV + 16, FEAT), jnp.bfloat16)] * QUERIES
    else:
        shapes = [
            jax.ShapeDtypeStruct((docs, FEAT), jnp.float32),
            jax.ShapeDtypeStruct((docs, BLOCK), jnp.float32),
        ]
    return pl.pallas_call(
        functools.partial(smooth_kernel, len(queries), len(cands), own, first_cands, last),
        in_specs=[smem] + [free] * (len(queries) + len(cands)) + [hbm] * (2 if last else 0),
        out_specs=[vmem if last else hbm] * len(shapes),
        out_shape=shapes,
        scratch_shapes=[
            pltpu.VMEM((docs, FEAT), jnp.float32),
            pltpu.VMEM((docs, BLOCK), jnp.float32),
            pltpu.VMEM((docs, EMB), jnp.bfloat16),
            pltpu.VMEM((len(cands) * DOCS_DEV, EMB + FEAT), jnp.bfloat16),
            pltpu.SemaphoreType.DMA((3 + len(queries) + len(cands),)),
        ],
        compiler_params=small(28),
        cost_estimate=pl.CostEstimate(
            flops=40 * 2 * BLOCK * BLOCK * (EMB + FEAT),
            bytes_accessed=sum(2 * v.size for v in (*queries, *cands)),
            transcendentals=40 * BLOCK * BLOCK,
        ),
        name="smooth_late" if last else "smooth_early",
    )(*operands)


def combine_kernel(*refs):
    parts, out = refs[:-1], refs[-1]
    top = parts[0][pl.ds(0, DOCS_DEV), :].astype(jnp.float32)
    sums = parts[0][pl.ds(DOCS_DEV, 16), :].astype(jnp.float32)
    for part in parts[1:]:
        top += part[pl.ds(0, DOCS_DEV), :].astype(jnp.float32)
        sums += part[pl.ds(DOCS_DEV, 16), :].astype(jnp.float32)
    bottom = sums[0:1, :] + sums[8:9, :]
    diagonal = lax.broadcasted_iota(jnp.int32, (BLOCK, BLOCK), 0) == lax.broadcasted_iota(
        jnp.int32, (BLOCK, BLOCK), 1
    )
    for b in range(NB_DEV):
        line = jnp.broadcast_to(bottom[:, b * BLOCK : (b + 1) * BLOCK], (BLOCK, BLOCK))
        column = jnp.sum(jnp.where(diagonal, line, 0.0), axis=1, keepdims=True)
        out[pl.ds(b * BLOCK, BLOCK), :] = (top[b * BLOCK : (b + 1) * BLOCK] / column).astype(jnp.bfloat16)


def steps(embeddings, features, candidates):
    partner_lists = send(candidates, y_of=partner_a)
    cand = cand_payload(embeddings, features)
    units = query_payload(cand, candidates, partner_lists)

    c_o, c_b = send(cand, dz=2), send(cand, y_of=partner_b)
    c_r, c_l = send(cand, dz=1), send(cand, dz=-1)
    c_br, c_bl = send(c_b, dz=1), send(c_b, dz=-1)
    c_bo = send(c_o, y_of=partner_b)
    q_r, q_l = send(units, dx=1), send(units, dx=-1)
    q_a, q_o = send(units, y_of=partner_a), send(units, dx=2)
    q_ar, q_al = send(q_a, dx=1), send(q_a, dx=-1)
    q_ao = send(q_o, y_of=partner_a)

    q_early, q_late = [q_r, q_l, q_a, q_o], [q_ar, q_al, q_ao]
    early, late = [cand, c_b, c_o, c_r, c_l, c_bo], [c_br, c_bl]
    early_other = [send(c, flip_core=True) for c in early]
    late_other = [send(c, flip_core=True) for c in late]

    codes = pair_codes(candidates, partner_lists, q_r, q_l, q_o)
    state = smooth(codes, q_early, early + early_other, 0, len(early), None)
    payloads = smooth(
        codes,
        q_early + q_late,
        late + late_other + early + early_other,
        2 * len(late),
        2 * len(late),
        state,
    )
    home = [
        dict(dx=-1), dict(dx=1), dict(y_of=partner_a), dict(dx=2),
        dict(dx=-1, y_of=partner_a), dict(dx=1, y_of=partner_a), dict(dx=2, y_of=partner_a),
    ]
    order = [6, 2, 4, 5, 3, 0, 1]
    back = [send(payloads[1 + i], **home[i]) for i in order]
    return pl.pallas_call(
        combine_kernel,
        in_specs=[pl.BlockSpec(memory_space=pltpu.VMEM)] * (1 + len(back)),
        out_shape=jax.ShapeDtypeStruct((DOCS_DEV, FEAT), jnp.bfloat16),
        compiler_params=pltpu.CompilerParams(vmem_limit_bytes=8 << 20),
        name="combine",
    )(payloads[0], *back)


def solution(mesh):
    spec = P(("row", "col"), None)
    return jax.shard_map(steps, mesh=mesh, in_specs=(spec, spec, spec), out_specs=spec, check_vma=False)
```

```python
import functools

import jax
import jax.numpy as jnp
from jax import lax
from jax.experimental import pallas as pl
from jax.experimental.pallas import tpu as pltpu
from jax.sharding import PartitionSpec as P


EMB = 1024
FEAT = 256
BLOCK = 128
NB_DEV = 2
BETA = 16
DOCS_DEV = NB_DEV * BLOCK
LIST_ROWS = 16
AXES = ("row", "col")
VALID, SELF = 1 << 11, 1 << 10
UNITS_VMEM = 67043328 - (1400 << 10)


def hop(dx=0, dz=0, flip_core=False, y_of=lambda y: y):
    pairs = []
    for x in range(4):
        for k in range(2):
            for z in range(4):
                for y in range(4):
                    x2, k2, z2, y2 = (x + dx) % 4, (1 - k if flip_core else k), (z + dz) % 4, y_of(y)
                    pairs.append(((2 * x + k) * 16 + 4 * z + y, (2 * x2 + k2) * 16 + 4 * z2 + y2))
    return pairs


def partner_a(y):
    return y ^ 1


def partner_b(y):
    return 3 - y


def send(value, **where):
    return lax.ppermute(value, AXES, hop(**where))


def units_kernel(emb_hbm, feat_hbm, list_hbm, unit_ref, cand_ref, emb_ref, list_ref, sems):
    copies = [
        pltpu.make_async_copy(emb_hbm, emb_ref, sems.at[0]),
        pltpu.make_async_copy(feat_hbm, cand_ref.at[:, pl.ds(EMB, FEAT)], sems.at[1]),
        pltpu.make_async_copy(list_hbm, list_ref, sems.at[2]),
    ]
    for copy in copies:
        copy.start()
    for copy in copies:
        copy.wait()
    values = emb_ref[...].astype(jnp.float32)
    factor = lax.rsqrt(jnp.mean(values * values, axis=1, keepdims=True) + 1e-06) * EMB ** (-0.5)
    units = (values * factor).astype(jnp.bfloat16)
    cand_ref[:, pl.ds(0, EMB)] = units
    unit_ref[pl.ds(0, DOCS_DEV), :] = units
    lists, length = list_ref.shape
    unit_ref[pl.ds(DOCS_DEV, LIST_ROWS), :] = jnp.zeros((LIST_ROWS, EMB), jnp.bfloat16)
    unit_ref[pl.ds(DOCS_DEV, lists), pl.ds(0, length)] = (
        list_ref[...].astype(jnp.float32).astype(jnp.bfloat16)
    )


def small(limit=8):
    return pltpu.CompilerParams(vmem_limit_bytes=limit << 20)


def unit_payloads(embeddings, features, candidates):
    return pl.pallas_call(
        units_kernel,
        in_specs=[pl.BlockSpec(memory_space=pltpu.HBM)] * 3,
        out_specs=(pl.BlockSpec(memory_space=pltpu.VMEM),) * 2,
        scratch_shapes=[
            pltpu.VMEM(embeddings.shape, embeddings.dtype),
            pltpu.VMEM(candidates.shape, candidates.dtype),
            pltpu.SemaphoreType.DMA((3,)),
        ],
        out_shape=(
            jax.ShapeDtypeStruct((DOCS_DEV + LIST_ROWS, EMB), jnp.bfloat16),
            jax.ShapeDtypeStruct((DOCS_DEV, EMB + FEAT), jnp.bfloat16),
        ),
        compiler_params=pltpu.CompilerParams(vmem_limit_bytes=UNITS_VMEM),
        name="units",
    )(embeddings, features, candidates)


Q_FROM = ((0, 0), (0, 1), (2, 0), (-1, 0), (1, 0), (2, 1), (-1, 1), (1, 1))
LATE_FROM, EARLY_FROM = ((-1, 1), (1, 1)), ((0, 0), (0, 1), (2, 0), (-1, 0), (1, 0), (2, 1))
C_FROM = tuple((core, *f) for group in (LATE_FROM, EARLY_FROM) for core in (0, 1) for f in group)
N_LATE, N_EARLY = 2 * len(LATE_FROM), 2 * len(EARLY_FROM)
OPENING, Q_OPENING = 3, 3
Q_EARLY, Q_LAST = 5, 6
PARTNER_ROW = tuple(i for i, (_, y) in enumerate(Q_FROM) if y)
OWN_ROW = tuple(i for i, (_, y) in enumerate(Q_FROM) if not y)
SLOTS, COUNT = 384, 376


def codes_kernel(length, wanted, *refs):
    query_refs, (out_ref, stage, lists, sems) = refs[:-4], refs[-4:]
    copies = [
        pltpu.make_async_copy(ref.at[pl.ds(DOCS_DEV, LIST_ROWS), pl.ds(0, BLOCK)], stage.at[i], sems.at[i])
        for i, ref in enumerate(query_refs)
    ]
    for copy in copies:
        copy.start()
    lists[...] = jnp.full_like(lists, -1.0)
    for copy in copies:
        copy.wait()
    for i in range(len(query_refs)):
        values = stage[i].astype(jnp.float32)
        lists[pl.ds(NB_DEV * i, NB_DEV), pl.ds(0, length)] = values[0:NB_DEV, 0:length]
    named = lists[...]
    queries = named.shape[0]

    row, col = lax.axis_index("row"), lax.axis_index("col")
    x, k, z, y = row >> 1, row & 1, col >> 2, col & 3
    lane = lax.broadcasted_iota(jnp.int32, (1, BLOCK), 1)
    ids = jnp.full((1, BLOCK), -2, jnp.int32)
    for i, (core, dz, partner) in enumerate(C_FROM):
        yy = 3 - y if partner else y
        kk = 1 - k if core else k
        device = (2 * x + kk) * 16 + ((z + dz) & 3) * 4 + yy
        ids = jnp.where((lane >> 1) == i, device * NB_DEV + (lane & 1), ids)

    blocks = lax.broadcasted_iota(jnp.int32, (queries, 256), 1).astype(jnp.float32)
    onehot = jnp.zeros((queries, 256), jnp.float32)
    for i in range(length):
        onehot = jnp.where(named[:, i : i + 1] == blocks, 1.0, onehot)
    chosen = jnp.where(lax.broadcasted_iota(jnp.int32, (256, BLOCK), 0) == ids, 1.0, 0.0)
    member = jnp.dot(
        onehot.astype(jnp.bfloat16), chosen.astype(jnp.bfloat16), preferred_element_type=jnp.float32
    )
    ahead = jnp.where(
        lax.broadcasted_iota(jnp.int32, (BLOCK, BLOCK), 0) < lax.broadcasted_iota(jnp.int32, (BLOCK, BLOCK), 1),
        1.0,
        0.0,
    ).astype(jnp.bfloat16)
    above = jnp.where(
        lax.broadcasted_iota(jnp.int32, (queries, queries), 0)
        > lax.broadcasted_iota(jnp.int32, (queries, queries), 1),
        1.0,
        0.0,
    ).astype(jnp.bfloat16)
    query = lax.broadcasted_iota(jnp.int32, (queries, BLOCK), 0)
    cand = lax.broadcasted_iota(jnp.int32, (queries, BLOCK), 1)
    late_end, half = N_LATE * NB_DEV, (N_LATE + N_EARLY // 2) * NB_DEV
    own_late = N_LATE // 2 * NB_DEV
    last_other = half + OPENING * NB_DEV
    opened_cand = jnp.logical_or(
        jnp.logical_and(cand >= late_end, cand < late_end + OPENING * NB_DEV),
        jnp.logical_and(cand >= half, cand < last_other),
    )
    early_cand = cand >= late_end
    middle = jnp.logical_and(early_cand, cand < last_other)
    opened = jnp.logical_and(query < Q_OPENING * NB_DEV, opened_cand)
    none = cand < 0
    partner_row = none
    for i in PARTNER_ROW:
        partner_row = jnp.logical_or(partner_row, (query >> 1) == i)
    own_row = jnp.logical_not(partner_row)
    before_last = query < Q_LAST * NB_DEV
    late_halves = (cand < own_late, jnp.logical_and(cand >= own_late, cand < late_end))
    calls = (
        (opened, none),
        (jnp.logical_and(jnp.logical_and(query < Q_EARLY * NB_DEV, middle), jnp.logical_not(opened)), none),
        (
            jnp.logical_and(jnp.logical_and(query >= Q_EARLY * NB_DEV, before_last), middle),
            jnp.logical_and(before_last, cand >= last_other),
        ),
        (jnp.logical_and(jnp.logical_not(before_last), early_cand), none),
        tuple(jnp.logical_and(partner_row, part) for part in late_halves),
        (jnp.logical_and(own_row, cand < late_end), none),
    )
    slot = lax.broadcasted_iota(jnp.int32, (1, SLOTS), 1)
    slots = slot.astype(jnp.float32)
    places = (N_LATE + N_EARLY) * NB_DEV
    place = lax.broadcasted_iota(jnp.int32, (places, 1), 0)
    for row_out, call in enumerate(wanted):
        groups = calls[call]
        base = jnp.zeros((1, 1), jnp.float32)
        position = jnp.full((queries, BLOCK), -1.0, jnp.float32)
        totals = []
        for group in groups:
            inside = jnp.where(group, member, 0.0)
            bits = inside.astype(jnp.bfloat16)
            in_row = jnp.dot(bits, ahead, preferred_element_type=jnp.float32)
            rows_above = jnp.sum(
                jnp.dot(above, bits, preferred_element_type=jnp.float32), axis=1, keepdims=True
            )
            position = jnp.where(inside > 0.0, base + rows_above + in_row, position)
            base = base + jnp.sum(jnp.sum(inside, axis=1, keepdims=True), axis=0, keepdims=True)
            totals.append(base)
        by_cand = jnp.concatenate(
            [position, jnp.full((BLOCK - queries, BLOCK), -1.0, jnp.float32)], axis=0
        ).T
        found = jnp.zeros((places, SLOTS), jnp.float32)
        for q in range(queries):
            code = q + 32 * place + VALID
            if q < NB_DEV:
                code = code + jnp.where(place == late_end + q, SELF, 0)
            found = jnp.where(by_cand[0:places, q : q + 1] == slots, code.astype(jnp.float32), found)
        line = jnp.sum(found, axis=0, keepdims=True)
        line = jnp.where(slot == COUNT, totals[1], jnp.where(slot == COUNT + 1, totals[0], line))
        out_ref[pl.ds(row_out, 1), :] = line.astype(jnp.int32)


def pair_codes(length, queries, wanted):
    return pl.pallas_call(
        functools.partial(codes_kernel, length, wanted),
        in_specs=[pl.BlockSpec(memory_space=pl.ANY)] * len(queries),
        out_specs=pl.BlockSpec(memory_space=pltpu.VMEM),
        out_shape=jax.ShapeDtypeStruct((len(wanted), SLOTS), jnp.int32),
        scratch_shapes=[
            pltpu.VMEM((len(queries), LIST_ROWS, BLOCK), jnp.bfloat16),
            pltpu.VMEM((len(Q_FROM) * NB_DEV, BLOCK), jnp.float32),
            pltpu.SemaphoreType.DMA((len(queries),)),
        ],
        compiler_params=small(),
        name="codes",
    )(*queries)


UNROLL = 8


def smooth_kernel(opens, row, q_slots, c_slots, waited, sent, *refs):
    codes, refs = refs[0], refs[1:]
    nq, nc = len(q_slots), len(c_slots)
    q_in, c_in = refs[:nq], refs[nq : nq + nc]
    at = nq + nc + (0 if opens else 4)
    num, den, q_buf, c_buf = refs[at : at + 4]
    payloads, sems = refs[at + 4 : -1], refs[-1]
    copies = []

    def load(source, target):
        copies.append(pltpu.make_async_copy(source, target, sems.at[len(copies)]))
        copies[-1].start()

    if opens:
        load(c_in[0].at[:, pl.ds(0, EMB)], q_buf.at[pl.ds(0, DOCS_DEV), :])
    for slot, ref in zip(q_slots, q_in):
        load(ref.at[pl.ds(0, DOCS_DEV), :], q_buf.at[pl.ds(slot * DOCS_DEV, DOCS_DEV), :])
    for slot, ref in zip(c_slots, c_in):
        load(ref, c_buf.at[pl.ds(slot * DOCS_DEV, DOCS_DEV), :])
    if opens:
        num[...] = jnp.zeros_like(num)
        den[...] = jnp.zeros_like(den)
    for copy in copies[:waited]:
        copy.wait()
    diagonal = lax.broadcasted_iota(jnp.int32, (BLOCK, BLOCK), 0) == lax.broadcasted_iota(
        jnp.int32, (BLOCK, BLOCK), 1
    )

    def turn(i, carry, unroll=UNROLL):
        pairs = []
        for u in range(unroll):
            code = codes[row, i * UNROLL + u]
            at_q = pl.ds(pl.multiple_of((code & 31) * BLOCK, BLOCK), BLOCK)
            at_c = pl.ds(pl.multiple_of(((code >> 5) & 31) * BLOCK, BLOCK), BLOCK)
            pairs.append((code, at_q, at_c))
        cosines = [
            lax.dot_general(
                q_buf[at_q, :],
                c_buf[at_c, pl.ds(0, EMB)],
                (((1,), (1,)), ((), ())),
                preferred_element_type=jnp.float32,
            )
            for _, at_q, at_c in pairs
        ]
        weights = []
        for (code, _, _), cosine in zip(pairs, cosines):
            weight = jnp.exp(BETA * (cosine - 1.0))
            drop = jnp.logical_or(code < VALID, jnp.logical_and((code & SELF) > 0, diagonal))
            weights.append(jnp.where(drop, 0.0, weight))
        terms = [
            jnp.dot(
                weight.astype(jnp.bfloat16),
                c_buf[at_c, pl.ds(EMB, FEAT)],
                preferred_element_type=jnp.float32,
            )
            for (_, _, at_c), weight in zip(pairs, weights)
        ]
        for (_, at_q, _), weight, term in zip(pairs, weights, terms):
            den[at_q, :] += weight
            num[at_q, :] += term
        return carry

    ready, count = codes[row, COUNT + 1] // UNROLL, codes[row, COUNT]
    if waited < len(copies):
        lax.fori_loop(0, ready, turn, 0)
        for copy in copies[waited:]:
            copy.wait()
    else:
        ready = 0
    whole = (count + UNROLL // 2 - 1) // UNROLL
    lax.fori_loop(ready, whole, turn, 0)

    @pl.when(count > whole * UNROLL)
    def _():
        turn(whole, 0, UNROLL // 2)

    if not payloads:
        return
    ones = jnp.ones((8, BLOCK), jnp.bfloat16)

    def lane_sums(part):
        return lax.dot_general(ones, part, (((1,), (1,)), ((), ())), preferred_element_type=jnp.float32)

    for i, payload in zip(sent, payloads):
        docs = pl.ds(i * DOCS_DEV, DOCS_DEV)
        payload[pl.ds(0, DOCS_DEV), :] = num[docs, :].astype(jnp.bfloat16)
        weights = den[docs, :]
        high = weights.astype(jnp.bfloat16)
        middle = (weights - high.astype(jnp.float32)).astype(jnp.bfloat16)
        sums = lane_sums(high) + lane_sums(middle)
        high = sums.astype(jnp.bfloat16).astype(jnp.float32)
        pair = jnp.concatenate([high, sums - high], axis=0).astype(jnp.bfloat16)
        payload[pl.ds(DOCS_DEV, 16), :] = pair


def smooth(codes, row, queries, q_slots, cands, c_slots, waited=99, state=(), sent=()):
    docs = len(Q_FROM) * DOCS_DEV
    free, vmem, smem = (pl.BlockSpec(memory_space=space) for space in (pl.ANY, pltpu.VMEM, pltpu.SMEM))
    loaded = [*queries, *cands]
    operands = [codes, *loaded, *state]
    shapes = [
        jax.ShapeDtypeStruct((docs, FEAT), jnp.float32),
        jax.ShapeDtypeStruct((docs, BLOCK), jnp.float32),
        jax.ShapeDtypeStruct((docs, EMB), jnp.bfloat16),
        jax.ShapeDtypeStruct((len(C_FROM) * DOCS_DEV, EMB + FEAT), jnp.bfloat16),
    ]
    shapes += [jax.ShapeDtypeStruct((DOCS_DEV + 16, FEAT), jnp.bfloat16)] * len(sent)
    return pl.pallas_call(
        functools.partial(smooth_kernel, not state, row, tuple(q_slots), tuple(c_slots), waited, sent),
        in_specs=[smem] + [free] * len(loaded) + [vmem] * len(state),
        out_specs=[vmem] * len(shapes),
        out_shape=shapes,
        input_output_aliases={1 + len(loaded) + i: i for i in range(len(state))},
        scratch_shapes=[pltpu.SemaphoreType.DMA((1 + len(loaded),))],
        compiler_params=small(),
        cost_estimate=pl.CostEstimate(
            flops=15 * 2 * BLOCK * BLOCK * (EMB + FEAT),
            bytes_accessed=sum(2 * v.size for v in loaded),
            transcendentals=15 * BLOCK * BLOCK,
        ),
    )(*operands)


def combine_kernel(*refs):
    parts, out = refs[:-1], refs[-1]
    top = parts[0][pl.ds(0, DOCS_DEV), :].astype(jnp.float32)
    sums = parts[0][pl.ds(DOCS_DEV, 16), :].astype(jnp.float32)
    for part in parts[1:]:
        top += part[pl.ds(0, DOCS_DEV), :].astype(jnp.float32)
        sums += part[pl.ds(DOCS_DEV, 16), :].astype(jnp.float32)
    bottom = sums[0:1, :] + sums[8:9, :]
    diagonal = lax.broadcasted_iota(jnp.int32, (BLOCK, BLOCK), 0) == lax.broadcasted_iota(
        jnp.int32, (BLOCK, BLOCK), 1
    )
    for b in range(NB_DEV):
        line = jnp.broadcast_to(bottom[:, b * BLOCK : (b + 1) * BLOCK], (BLOCK, BLOCK))
        column = jnp.sum(jnp.where(diagonal, line, 0.0), axis=1, keepdims=True)
        out[pl.ds(b * BLOCK, BLOCK), :] = (top[b * BLOCK : (b + 1) * BLOCK] / column).astype(jnp.bfloat16)


def steps(embeddings, features, candidates):
    units, cand = unit_payloads(embeddings, features, candidates)

    c_o, c_b = send(cand, dz=2), send(cand, y_of=partner_b)
    c_r, c_l = send(cand, dz=1), send(cand, dz=-1)
    c_br, c_bl = send(c_b, dz=1), send(c_b, dz=-1)
    c_bo = send(c_o, y_of=partner_b)
    q_r, q_l = send(units, dx=1), send(units, dx=-1)
    q_a, q_o = send(units, y_of=partner_a), send(units, dx=2)
    q_ar, q_al = send(q_a, dx=1), send(q_a, dx=-1)
    q_ao = send(q_o, y_of=partner_a)

    queries = [units, q_a, q_o, q_r, q_l, q_ao, q_ar, q_al]
    early, late = [cand, c_b, c_o, c_r, c_l, c_bo], [c_br, c_bl]
    early += [send(c, flip_core=True) for c in early]
    late += [send(c, flip_core=True) for c in late]
    length = candidates.shape[1]

    half = len(early) // 2
    first = [*range(OPENING), *range(half, half + OPENING)]
    middle, last = range(OPENING, half), range(half + OPENING, len(early))

    def placed(chosen):
        return [early[i] for i in chosen], [N_LATE + i for i in chosen]

    def codes_of(known, *calls):
        return pair_codes(length, queries[:known], calls)

    def call(codes, row, first_query, end_query, chosen, waited, state, sent=()):
        cands, c_slots = placed(chosen) if chosen is not late else (late, range(N_LATE))
        q_slots = range(first_query, end_query)
        out = smooth(codes, row, [queries[i] for i in q_slots], q_slots, cands, c_slots, waited, state, sent)
        return out[:4], out[4:]

    codes = codes_of(Q_OPENING, 0)
    state, _ = call(codes, 0, 1, Q_OPENING, first, 99, ())
    codes = codes_of(Q_EARLY, 1)
    state, _ = call(codes, 0, Q_OPENING, Q_EARLY, middle, 99, state)
    codes = codes_of(Q_LAST, 2)
    state, _ = call(codes, 0, Q_EARLY, Q_LAST, last, Q_LAST - Q_EARLY, state)
    codes = codes_of(len(queries), 3, 4, 5)
    state, _ = call(codes, 0, Q_LAST, len(queries), [], 99, state)
    state, far = call(codes, 1, 0, 0, late, N_LATE // 2, state, PARTNER_ROW)
    state, near = call(codes, 2, 0, 0, [], 99, state, OWN_ROW)
    payloads = {**dict(zip(PARTNER_ROW, far)), **dict(zip(OWN_ROW, near))}
    home = [
        dict(y_of=partner_a), dict(dx=2), dict(dx=-1), dict(dx=1),
        dict(dx=2, y_of=partner_a), dict(dx=-1, y_of=partner_a), dict(dx=1, y_of=partner_a),
    ]
    order = [0, 4, 5, 6, 1, 2, 3]
    back = [send(payloads[1 + i], **home[i]) for i in order]
    return pl.pallas_call(
        combine_kernel,
        in_specs=[pl.BlockSpec(memory_space=pltpu.VMEM)] * (1 + len(back)),
        out_shape=jax.ShapeDtypeStruct((DOCS_DEV, FEAT), jnp.bfloat16),
        compiler_params=pltpu.CompilerParams(vmem_limit_bytes=8 << 20),
        name="combine",
    )(payloads[0], *back)


def solution(mesh):
    spec = P(("row", "col"), None)
    return jax.shard_map(steps, mesh=mesh, in_specs=(spec, spec, spec), out_specs=spec, check_vma=False)
```
